32 devices in a mesh: groups: 2 (over x), dom: 16 (over z, y, core).
Axes of the slice: x: 2, y: 2, z: 4, core: 2. Of those that a mesh axis runs over, the one named last changes fastest.
Arguments:
- node_latent: bfloat16 [32768, 128], P(('groups', 'dom')), parts along dimension 0, may hold values from -6 to 6
- edge_latent: bfloat16 [196608, 128], P(('groups', 'dom')), parts along dimension 0, may hold values from -6 to 6
- node_cot: bfloat16 [32768, 128], P(('groups', 'dom')), parts along dimension 0, may hold values from -6 to 6
- edge_cot: bfloat16 [196608, 128], P(('groups', 'dom')), parts along dimension 0, may hold values from -6 to 6
- base_pos: float32 [3, 32768], P(None, ('groups', 'dom')), parts along dimension 1
- centers: float32 [3, 2048], replicated, may hold values from 0 to 1
- amplitudes: float32 [3, 2048], replicated, may hold values from -0.3 to 0.3
- edge_in: bfloat16 [384, 128], replicated, may hold values from -0.3125 to 0.3125
- edge_geo: float32 [4, 128], replicated, may hold values from -3 to 3
- edge_out: bfloat16 [128, 128], replicated, may hold values from -0.5 to 0.5
- edge_gain: float32 [128], replicated, may hold values from 0.5 to 1.5
- node_in: bfloat16 [256, 128], replicated, may hold values from -0.375 to 0.375
- node_out: bfloat16 [128, 128], replicated, may hold values from -0.5 to 0.5
- node_gain: float32 [128], replicated, may hold values from 0.5 to 1.5
- senders: int32 [196608], P(('groups', 'dom')), parts along dimension 0, may hold values from 0 to 3071, as said below
- receivers: int32 [196608], P(('groups', 'dom')), parts along dimension 0, may hold values from 0 to 1023
- send_rows: int32 [32, 16, 128], P(('groups', 'dom')), parts along dimension 0, may hold values from 0 to 1023
Outputs:
- grad_nodes: float32 [32768, 128], P(('groups', 'dom')), parts along dimension 0
- grad_edges: float32 [196608, 128], P(('groups', 'dom')), parts along dimension 0
- grad_controls: float32 [6, 2048], P('groups'), parts along dimension 0
The draws below stay inside these ranges and needn't reach their ends.
There are 2 independent parts, one for each index of `groups`. The reference program is written for one: setup_inputs(seed, part) draws one part's arguments, and reference() takes and returns one part's arrays. A program takes and returns all parts, laid end to end along the dimension named above; an argument that names none is the same for every part. Nothing has to cross between parts.
Inputs may be any that keep to these rules, and one draw needn't show every extreme that they name: `senders`: for edge j in partition q = j // 6144: a value below 1024 is an own node; a value v of 1024 or more names slot (v - 1024) % 128 of the block from partition p = (v - 1024) // 128, and 1 <= |p - q| <= 2. Every partition has an edge using slot 127 of some block.
All inputs are finite; a program needn't handle non-finite values.
Results may differ from the reference program's by a relative error of at most 0.0085.
Values may be sent and summed in bfloat16 or wider, within the bound.
A program may use at most 128 MiB of HBM per device.

```python
import jax
import jax.numpy as jnp
from jax import lax

LATENT = 128
CTRL = 2048
NV_DEV = 1024
HALO = 128
REACH = 2
NE_DEV = 6144
NODES = 16384
EDGES = 98304
N_DOM = 16


def draw_base_pos(key, part):
    uniform_draw = jax.random.uniform(jax.random.fold_in(key, 3), (3, NODES), jnp.float32)
    owner = (jnp.arange(NODES, dtype=jnp.int32) // NV_DEV).astype(jnp.float32)
    across = (owner + uniform_draw[0]) / N_DOM
    second = uniform_draw[1]
    third = uniform_draw[2]
    return jnp.stack([across, second, third], axis=0).astype(jnp.float32)


def draw_senders(key, part):
    keys = jax.random.split(jax.random.fold_in(key, 11), 6)
    edge_ids = jnp.arange(EDGES, dtype=jnp.int32)
    owner = edge_ids // NE_DEV
    within = edge_ids % NE_DEV
    local_pick = jax.random.randint(keys[0], (EDGES,), 0, NV_DEV, dtype=jnp.int32)
    share = jax.random.randint(keys[1], (N_DOM,), 10, 50, dtype=jnp.int32)
    dice = jax.random.randint(keys[2], (EDGES,), 0, 100, dtype=jnp.int32)
    first = within == 0
    choose = jnp.where(first, 0, jax.random.randint(keys[3], (EDGES,), 0, 2 * REACH, dtype=jnp.int32))
    offset_val = jnp.where(choose < REACH, choose - REACH, choose - REACH + 1)
    source = owner + offset_val
    source = jnp.where((source >= 0) & (source < N_DOM), source, owner - offset_val)
    capacity = jax.random.randint(keys[4], (N_DOM, 2 * REACH), HALO // 4, HALO + 1, dtype=jnp.int32)
    limit = jnp.where(choose == 0, HALO, capacity[owner, choose])
    slot_pick = jax.random.randint(keys[5], (EDGES,), 0, 1 << 20, dtype=jnp.int32) % limit
    slot_pick = jnp.where(first, HALO - 1, slot_pick)
    remote = (dice < share[owner]) | first
    return jnp.where(remote, NV_DEV + source * HALO + slot_pick, local_pick).astype(jnp.int32)


def place_ends(array, stream_key, low, top_value):
    index_at = [jax.random.randint(jax.random.fold_in(stream_key, axis), (), 0, length) for axis, length in enumerate(array.shape)]
    widest = array.shape.index(max(array.shape))
    next_to = index_at[:widest] + [(index_at[widest] + 1) % array.shape[widest]] + index_at[widest + 1:]
    return array.at[tuple(index_at)].set(low).at[tuple(next_to)].set(top_value)


def block_levels(key, shape, cuts, smallest, largest):
    level = 1.0
    for axis_at, shards_of in cuts:
        draws = jax.random.uniform(jax.random.fold_in(jax.random.fold_in(key, 6), axis_at), (shards_of,), jnp.float32, smallest / len(cuts), largest / len(cuts))
        level = level * jnp.repeat(jnp.exp(draws), shape[axis_at] // shards_of).reshape((-1,) + (1,) * (len(shape) - 1 - axis_at))
    return level


def normal_values(key, dims, scale, most, cuts=(), held_as=jnp.bfloat16):
    result = jax.random.normal(key, dims, jnp.float32) * scale
    if len(cuts) > 0:
        result = block_levels(key, dims, cuts, -0.22, 0.18) * result
    return jnp.clip(result, min=-most, max=most).astype(held_as)


def setup_inputs(seed: int = 0, part: int = 0) -> dict:
    key_of = jax.random.split(jax.random.key(seed), 18)
    own_keys = jax.random.split(jax.random.fold_in(key_of[17], part), 18)
    node_latent = normal_values(own_keys[0], (NODES, LATENT), 1.0, 6.0, ((0, 16),))
    edge_latent = normal_values(own_keys[1], (EDGES, LATENT), 1.0, 6.0, ((0, 16),))
    node_cot = normal_values(own_keys[2], (NODES, LATENT), 1.0, 6.0, ((0, 16),))
    edge_cot = normal_values(own_keys[3], (EDGES, LATENT), 1.0, 6.0, ((0, 16),))
    base_pos = draw_base_pos(jax.random.fold_in(jax.random.fold_in(key_of[17], part), 71), part)
    centers = jnp.clip(jax.random.uniform(key_of[5], (3, CTRL), jnp.float32, 0.0, 1.0), 0.0, 1.0)
    amplitudes = normal_values(key_of[6], (3, CTRL), 0.05, 0.3, (), jnp.float32)
    edge_in = normal_values(key_of[7], (3 * LATENT, LATENT), (3 * LATENT) ** -0.5, 0.3125)
    edge_geo = normal_values(key_of[8], (4, LATENT), 4 ** -0.5, 3.0, (), jnp.float32)
    edge_out = normal_values(key_of[9], (LATENT, LATENT), LATENT ** -0.5, 0.5)
    edge_gain = jnp.clip(1.0 + 0.1 * jax.random.normal(key_of[10], (LATENT,), jnp.float32), 0.5, 1.5)
    node_in = normal_values(key_of[11], (2 * LATENT, LATENT), (2 * LATENT) ** -0.5, 0.375)
    node_out = normal_values(key_of[12], (LATENT, LATENT), LATENT ** -0.5, 0.5)
    node_gain = jnp.clip(1.0 + 0.1 * jax.random.normal(key_of[13], (LATENT,), jnp.float32), 0.5, 1.5)
    senders = draw_senders(jax.random.fold_in(jax.random.fold_in(key_of[17], part), 71), part)
    receivers = place_ends(jax.random.randint(own_keys[15], (EDGES,), 0, NV_DEV), jax.random.fold_in(own_keys[15], 1), 0, NV_DEV - 1).astype(jnp.int32)
    send_rows = place_ends(jax.random.randint(own_keys[16], (N_DOM, N_DOM, HALO), 0, NV_DEV), jax.random.fold_in(own_keys[16], 1), 0, NV_DEV - 1).astype(jnp.int32)
    return dict(node_latent=node_latent, edge_latent=edge_latent, node_cot=node_cot, edge_cot=edge_cot, base_pos=base_pos, centers=centers, amplitudes=amplitudes, edge_in=edge_in, edge_geo=edge_geo, edge_out=edge_out, edge_gain=edge_gain, node_in=node_in, node_out=node_out, node_gain=node_gain, senders=senders, receivers=receivers, send_rows=send_rows)


RBF_RATE = 78.125
exact_mode = lax.Precision.HIGHEST

def radial(points, centers):
    squared = jnp.zeros((points.shape[1], centers.shape[1]), jnp.float32)
    for component in range(3):
        offset_k = points[component][:, None] - centers[component][None, :]
        squared = squared + offset_k * offset_k
    return jnp.exp(-RBF_RATE * squared)

def layer_norm(values, gain):
    centred = values - lax.optimization_barrier(jnp.mean(values, axis=-1, keepdims=True))
    spread_inv = lax.rsqrt(lax.optimization_barrier(jnp.mean(centred * centred, axis=-1, keepdims=True)) + 1e-05)
    return centred * spread_inv * gain

def norm_back(values, gain, upstream):
    centred = values - lax.optimization_barrier(jnp.mean(values, axis=-1, keepdims=True))
    spread_inv = lax.rsqrt(lax.optimization_barrier(jnp.mean(centred * centred, axis=-1, keepdims=True)) + 1e-05)
    normed = centred * spread_inv
    scaled = upstream * gain
    return spread_inv * (scaled - lax.optimization_barrier(jnp.mean(scaled, axis=-1, keepdims=True)) - normed * lax.optimization_barrier(jnp.mean(scaled * normed, axis=-1, keepdims=True)))

def silu_slope(values):
    sigma = jax.nn.sigmoid(values)
    return sigma * (1.0 + values * (1.0 - sigma))

def reference(node_latent, edge_latent, node_cot, edge_cot, base_pos, centers, amplitudes, edge_in, edge_geo, edge_out, edge_gain, node_in, node_out, node_gain, senders, receivers, send_rows):
    width = node_latent.shape[1]
    edge_ids = jnp.arange(EDGES, dtype=jnp.int32)
    edge_home = (edge_ids // NE_DEV).astype(jnp.int32)
    recv_global = (edge_home * NV_DEV + receivers).astype(jnp.int32)
    is_local = senders < NV_DEV
    slot_index = jnp.maximum(senders - NV_DEV, 0).astype(jnp.int32)
    source_part = jnp.minimum(slot_index // HALO, N_DOM - 1).astype(jnp.int32)
    halo_row = send_rows[source_part, edge_home, slot_index % HALO]
    send_global = jnp.where(is_local, edge_home * NV_DEV + senders, source_part * NV_DEV + halo_row).astype(jnp.int32)
    base_blocks = jnp.transpose(base_pos.reshape(3, N_DOM, NV_DEV), (1, 0, 2))

    def place_block(block):
        return block + jnp.einsum('kc,nc->kn', amplitudes, radial(block, centers), precision=exact_mode)
    placed = jnp.transpose(lax.map(place_block, base_blocks), (1, 0, 2)).reshape(3, NODES)
    w_send = edge_in[:width]
    w_recv = edge_in[width:2 * width]
    w_edge = edge_in[2 * width:]
    w_node = node_in[:width]
    w_agg = node_in[width:]
    h_send = node_latent[send_global]
    h_recv = node_latent[recv_global]
    delta = placed[:, send_global] - placed[:, recv_global]
    length = jnp.sqrt(lax.optimization_barrier(jnp.sum(delta * delta, axis=0)) + 0.01)
    geometry = jnp.concatenate([delta, length[None, :]], axis=0)
    pre_act = jnp.dot(h_send, w_send, preferred_element_type=jnp.float32) + jnp.dot(h_recv, w_recv, preferred_element_type=jnp.float32) + jnp.dot(edge_latent, w_edge, preferred_element_type=jnp.float32) + jnp.einsum('ke,kl->el', geometry, edge_geo, precision=exact_mode)
    hidden = jax.nn.silu(pre_act).astype(jnp.bfloat16)
    edge_mid = jnp.dot(hidden, edge_out, preferred_element_type=jnp.float32)
    updated = (edge_latent.astype(jnp.float32) + layer_norm(edge_mid, edge_gain)).astype(jnp.bfloat16)
    aggregate = jax.ops.segment_sum(updated.astype(jnp.float32), recv_global, NODES).astype(jnp.bfloat16)
    node_pre = jnp.dot(node_latent, w_node, preferred_element_type=jnp.float32) + jnp.dot(aggregate, w_agg, preferred_element_type=jnp.float32)
    node_hidden = jax.nn.silu(node_pre).astype(jnp.bfloat16)
    node_mid = jnp.dot(node_hidden, node_out, preferred_element_type=jnp.float32)
    grad_mid = norm_back(node_mid, node_gain, node_cot.astype(jnp.float32)).astype(jnp.bfloat16)
    grad_pre = (jnp.dot(grad_mid, node_out.T, preferred_element_type=jnp.float32) * silu_slope(node_pre)).astype(jnp.bfloat16)
    grad_agg = jnp.dot(grad_pre, w_agg.T, preferred_element_type=jnp.float32).astype(jnp.bfloat16)
    grad_upd = edge_cot.astype(jnp.float32) + grad_agg[recv_global].astype(jnp.float32)
    grad_emid = norm_back(edge_mid, edge_gain, grad_upd).astype(jnp.bfloat16)
    grad_epre = jnp.dot(grad_emid, edge_out.T, preferred_element_type=jnp.float32) * silu_slope(pre_act)
    grad_eb = grad_epre.astype(jnp.bfloat16)
    grad_edges = grad_upd + jnp.dot(grad_eb, w_edge.T, preferred_element_type=jnp.float32)
    grad_snd = jnp.dot(grad_eb, w_send.T, preferred_element_type=jnp.float32).astype(jnp.bfloat16)
    grad_rcv = jnp.dot(grad_eb, w_recv.T, preferred_element_type=jnp.float32).astype(jnp.bfloat16)
    grad_geo = jnp.einsum('el,kl->ke', grad_epre, edge_geo, precision=exact_mode)
    grad_delta = grad_geo[:3] + grad_geo[3][None, :] * delta / length[None, :]
    grad_nodes = node_cot.astype(jnp.float32) + jnp.dot(grad_pre, w_node.T, preferred_element_type=jnp.float32) + jax.ops.segment_sum(grad_snd.astype(jnp.float32), send_global, NODES) + jax.ops.segment_sum(grad_rcv.astype(jnp.float32), recv_global, NODES)
    grad_pos = jax.ops.segment_sum(grad_delta.T, send_global, NODES).T - jax.ops.segment_sum(grad_delta.T, recv_global, NODES).T
    grad_blocks = jnp.transpose(grad_pos.reshape(3, N_DOM, NV_DEV), (1, 0, 2))

    def amp_block(pair):
        block, grads = pair
        return jnp.einsum('kn,nc->kc', grads, radial(block, centers), precision=exact_mode)
    grad_controls = lax.optimization_barrier(jnp.sum(lax.map(amp_block, (base_blocks, grad_blocks)), axis=0))
    return (grad_nodes, grad_edges, grad_controls)
```

```python
import functools

import jax
import jax.numpy as jnp
from jax import lax
from jax.experimental import pallas as pl
from jax.experimental.pallas import tpu as pltpu
from jax.sharding import PartitionSpec as P

REACH = 2
RBF_RATE = 78.125
OFFSETS = [step for step in range(-REACH, REACH + 1) if step != 0]
NEAR = len(OFFSETS)
F32 = jnp.float32
BF16 = jnp.bfloat16
VMEM_FULL = pl.BlockSpec(memory_space=pltpu.VMEM)


def dot(a, b):
    return jnp.dot(a, b, preferred_element_type=F32)


def dot_t(a, b):
    return lax.dot_general(a, b, (((1,), (1,)), ((), ())), preferred_element_type=F32)


def stack_rows(rows, height):
    at = lax.broadcasted_iota(jnp.int32, (height, rows[0].shape[1]), 0)
    out = jnp.zeros(at.shape, F32)
    for k, row in enumerate(rows):
        out = jnp.where(at == k, row, out)
    return out


def split(x):
    hi = x.astype(BF16)
    return hi, (x - hi.astype(F32)).astype(BF16)


def columns_match(row, width):
    block = row.shape[1]
    spread = jnp.transpose(jnp.broadcast_to(row.astype(F32), (128, block)))
    lane = lax.broadcasted_iota(jnp.int32, (block, 128), 1).astype(F32)
    return jnp.concatenate(
        [
            jnp.where(spread - float(128 * j) == lane, 1.0, 0.0).astype(BF16)
            for j in range(width // 128)
        ],
        axis=1,
    )


def rows_match(row, height, first=0):
    at = lax.broadcasted_iota(jnp.int32, (height, row.shape[1]), 0) + first
    return jnp.where(at == row, 1.0, 0.0).astype(BF16)


def lanes_like(x):
    return lax.broadcasted_iota(jnp.int32, x.shape, 1)


def prepare_kernel(lat_ref, pos_ref, cen_ref, amp_ref, rows_ref, table_ref, out_ref, amp_s):
    step = pl.program_id(0)
    block = lat_ref.shape[0]

    @pl.when(step == 0)
    def _():
        hi, lo = split(amp_ref[...])
        hi, lo = hi.astype(F32), lo.astype(F32)
        rows = [hi[k : k + 1] for k in range(3)]
        zero = jnp.zeros_like(rows[0])
        rows = rows + [zero] + [lo[k : k + 1] for k in range(3)]
        amp_s[...] = stack_rows(rows, 128).astype(BF16)

    base = jnp.transpose(stack_rows([pos_ref[k : k + 1, :] for k in range(3)], 128))
    squared = None
    for k in range(3):
        off = base[:, k : k + 1] - cen_ref[k : k + 1, :]
        squared = off * off if squared is None else squared + off * off
    phi_hi, phi_lo = split(jnp.exp(-RBF_RATE * squared))
    moved = dot_t(phi_hi, amp_s[...]) + dot_t(phi_lo, amp_s[...])
    moved = moved + pltpu.roll(moved, 124, 1)
    lane = lanes_like(base)
    placed = jnp.where(lane < 3, base + moved, 0.0)
    hi = placed.astype(BF16).astype(F32)
    rest = placed - hi
    mid = rest.astype(BF16).astype(F32)
    low = (rest - mid).astype(BF16).astype(F32)
    parts = hi + pltpu.roll(mid, 4, 1) + pltpu.roll(low, 8, 1)
    at = pl.ds(pl.multiple_of(step * block, block), block)
    width = lat_ref.shape[1]
    table_ref[at, :width] = lat_ref[...]
    table_ref[at, width:] = parts.astype(BF16)

    @pl.when(step == pl.num_programs(0) - 1)
    def _():
        match = columns_match(rows_ref[...], table_ref.shape[0])
        out_ref[...] = dot(match, table_ref[...]).astype(BF16)


def prepare(node_latent, base_pos, centers, amplitudes, rows):
    nodes, width = node_latent.shape
    block = 256
    count = rows.shape[1]
    full = lambda shape: pl.BlockSpec(shape, lambda i: (0,) * len(shape))
    return pl.pallas_call(
        prepare_kernel,
        grid=(nodes // block,),
        in_specs=[
            pl.BlockSpec((block, width), lambda i: (i, 0)),
            pl.BlockSpec((3, block), lambda i: (0, i)),
            full(centers.shape),
            full(amplitudes.shape),
            full(rows.shape),
        ],
        out_specs=[full((nodes, width + 128)), full((count, width + 128))],
        out_shape=[
            jax.ShapeDtypeStruct((nodes, width + 128), BF16),
            jax.ShapeDtypeStruct((count, width + 128), BF16),
        ],
        scratch_shapes=[pltpu.VMEM((128, centers.shape[1]), BF16)],
        compiler_params=pltpu.CompilerParams(dimension_semantics=("arbitrary",)),
        name="prepare",
    )(node_latent, base_pos, centers, amplitudes, rows)


def exchange_kernel(parts, x_ref, o_ref, send_sem, recv_sem):
    me = lax.axis_index("dom")
    partners = [lax.rem(me + off + parts, parts) for off in OFFSETS]
    barrier = pltpu.get_barrier_semaphore()
    for partner in partners:
        pl.semaphore_signal(
            barrier, inc=1, device_id={"dom": partner}, device_id_type=pl.DeviceIdType.MESH
        )
    pl.semaphore_wait(barrier, NEAR)
    copies = []
    for k, partner in enumerate(partners):
        there = NEAR - 1 - k
        copy = pltpu.make_async_remote_copy(
            src_ref=x_ref.at[k],
            dst_ref=o_ref.at[there],
            send_sem=send_sem.at[k],
            recv_sem=recv_sem.at[there],
            device_id={"dom": partner},
            device_id_type=pl.DeviceIdType.MESH,
        )
        copy.start()
        copies.append(copy)
    for copy in copies:
        copy.wait()


def exchange(blocks, parts, ident):
    return pl.pallas_call(
        functools.partial(exchange_kernel, parts),
        out_shape=jax.ShapeDtypeStruct(blocks.shape, blocks.dtype),
        in_specs=[VMEM_FULL],
        out_specs=VMEM_FULL,
        scratch_shapes=[pltpu.SemaphoreType.DMA((NEAR,)), pltpu.SemaphoreType.DMA((NEAR,))],
        compiler_params=pltpu.CompilerParams(collective_id=ident, has_side_effects=True),
        name=f"exchange_{ident}",
    )(blocks)


def total_kernel(parts, x_ref, o_ref, work, got, send_sem, recv_sem):
    steps = parts.bit_length() - 1
    me = lax.axis_index("dom")
    partners = []
    for s in range(steps):
        bit = lax.rem(me // (1 << s), 2)
        partners.append(me + (1 << s) * (1 - 2 * bit))
    barrier = pltpu.get_barrier_semaphore()
    for partner in partners:
        pl.semaphore_signal(
            barrier, inc=1, device_id={"dom": partner}, device_id_type=pl.DeviceIdType.MESH
        )
    pl.semaphore_wait(barrier, steps)
    for s, partner in enumerate(partners):
        source = x_ref if s == 0 else work.at[s - 1]
        copy = pltpu.make_async_remote_copy(
            src_ref=source,
            dst_ref=got.at[s],
            send_sem=send_sem.at[s],
            recv_sem=recv_sem.at[s],
            device_id={"dom": partner},
            device_id_type=pl.DeviceIdType.MESH,
        )
        copy.start()
        copy.wait()
        target = o_ref if s == steps - 1 else work.at[s]
        target[...] = source[...] + got[s]


def total(values, parts, ident):
    steps = parts.bit_length() - 1
    if parts != 1 << steps or steps == 0:
        return lax.psum(values, "dom")
    return pl.pallas_call(
        functools.partial(total_kernel, parts),
        out_shape=jax.ShapeDtypeStruct(values.shape, values.dtype),
        in_specs=[VMEM_FULL],
        out_specs=VMEM_FULL,
        scratch_shapes=[
            pltpu.VMEM((steps,) + values.shape, values.dtype),
            pltpu.VMEM((steps,) + values.shape, values.dtype),
            pltpu.SemaphoreType.DMA((steps,)),
            pltpu.SemaphoreType.DMA((steps,)),
        ],
        compiler_params=pltpu.CompilerParams(collective_id=ident, has_side_effects=True),
        name="total",
    )(values)


def normed_of(values):
    centred = values - jnp.mean(values, axis=-1, keepdims=True)
    inv = lax.rsqrt(jnp.mean(centred * centred, axis=-1, keepdims=True) + 1e-05)
    return centred * inv, inv


def norm_back(values, gain, upstream):
    normed, inv = normed_of(values)
    scaled = upstream * gain
    return inv * (
        scaled
        - jnp.mean(scaled, axis=-1, keepdims=True)
        - normed * jnp.mean(scaled * normed, axis=-1, keepdims=True)
    )


def silu_slope(values):
    sigma = jax.nn.sigmoid(values)
    return sigma * (1.0 + values * (1.0 - sigma))


def edges_kernel(
    sidx_ref,
    ridx_ref,
    table_ref,
    halo_ref,
    elat_ref,
    ecot_ref,
    ncot_ref,
    ein_ref,
    egeo_ref,
    eout_ref,
    egain_ref,
    nin_ref,
    nout_ref,
    ngain_ref,
    gedge_ref,
    gnode_ref,
    gpos_ref,
    back_ref,
    pre_s,
    mid_s,
    geo_s,
    agg_s,
    gagg_s,
    geo_rows,
    geo_cols,
    own_s,
    away_s,
    recv_s,
):
    phase = pl.program_id(0)
    step = pl.program_id(1)
    last = pl.num_programs(1) - 1
    nodes = table_ref.shape[0]
    block, width = elat_ref.shape
    away = halo_ref.shape[0]
    at = pl.ds(pl.multiple_of(step * block, block), block)
    srow = sidx_ref[0]
    rrow = ridx_ref[0]

    @pl.when((phase == 0) & (step == 0))
    def _():
        agg_s[...] = jnp.zeros_like(agg_s)
        own_s[...] = jnp.zeros_like(own_s)
        away_s[...] = jnp.zeros_like(away_s)
        recv_s[...] = jnp.zeros_like(recv_s)
        hi, lo = split(stack_rows([egeo_ref[k : k + 1, :] for k in range(4)], 128))
        geo_rows[...] = jnp.concatenate([hi, hi, lo], axis=0)
        geo_cols[...] = jnp.concatenate([hi, hi, lo], axis=1)

    @pl.when(phase == 0)
    def _():
        match = columns_match(srow, nodes + away)
        sent = dot(match[:, :nodes], table_ref[...]) + dot(match[:, nodes:], halo_ref[...])
        got = dot(columns_match(rrow, nodes), table_ref[...])
        apart = sent[:, width:] - got[:, width:]
        delta = apart + (pltpu.roll(apart, 124, 1) + pltpu.roll(apart, 120, 1))
        lane = lanes_like(delta)
        delta = jnp.where(lane < 3, delta, 0.0)
        length = jnp.sqrt(jnp.sum(delta * delta, axis=-1, keepdims=True) + 0.01)
        geo = jnp.where(lane == 3, length, delta)
        geo_hi, geo_lo = split(geo)
        latent = elat_ref[...]
        joined = jnp.concatenate(
            [sent[:, :width].astype(BF16), got[:, :width].astype(BF16), latent], axis=1
        )
        pre = dot(joined, ein_ref[...]) + dot(
            jnp.concatenate([geo_hi, geo_lo, geo_hi], axis=1), geo_rows[...]
        )
        hidden = (pre * jax.nn.sigmoid(pre)).astype(BF16)
        mid = dot(hidden, eout_ref[...])
        normed, _ = normed_of(mid)
        updated = (latent.astype(F32) + normed * egain_ref[...]).astype(BF16)
        agg_s[...] += dot(rows_match(rrow, nodes), updated)
        pre_s[at, :] = pre
        mid_s[at, :] = mid
        geo_s[at, :] = geo

    @pl.when((phase == 0) & (step == last))
    def _():
        latent = table_ref[:, :width]
        w_node = nin_ref[:width, :]
        w_agg = nin_ref[width:, :]
        cot = ncot_ref[...].astype(F32)
        node_pre = dot(latent, w_node) + dot(agg_s[...].astype(BF16), w_agg)
        node_hidden = (node_pre * jax.nn.sigmoid(node_pre)).astype(BF16)
        node_mid = dot(node_hidden, nout_ref[...])
        grad_mid = norm_back(node_mid, ngain_ref[...], cot).astype(BF16)
        grad_pre = (dot_t(grad_mid, nout_ref[...]) * silu_slope(node_pre)).astype(BF16)
        gagg_s[...] = dot_t(grad_pre, w_agg).astype(BF16)
        agg_s[...] = cot + dot_t(grad_pre, w_node)

    @pl.when(phase == 1)
    def _():
        pre = pre_s[at, :]
        mid = mid_s[at, :]
        geo = geo_s[at, :]
        grad_upd = ecot_ref[...].astype(F32) + dot(columns_match(rrow, nodes), gagg_s[...])
        grad_mid = norm_back(mid, egain_ref[...], grad_upd).astype(BF16)
        grad_pre = dot_t(grad_mid, eout_ref[...]) * silu_slope(pre)
        hi, lo = split(grad_pre)
        back = dot_t(hi, ein_ref[...])
        gedge_ref[...] = grad_upd + back[:, 2 * width :]
        grad_geo = dot_t(jnp.concatenate([hi, lo, hi], axis=1), geo_cols[...])
        lane = lanes_like(geo)
        pick = lane == 3
        ratio = jnp.sum(jnp.where(pick, grad_geo, 0.0), axis=-1, keepdims=True) / jnp.sum(
            jnp.where(pick, geo, 0.0), axis=-1, keepdims=True
        )
        grad_delta = jnp.where(lane < 3, grad_geo + geo * ratio, 0.0)
        d_hi, d_lo = split(grad_delta)
        parts = (d_hi.astype(F32) + pltpu.roll(d_lo.astype(F32), 4, 1)).astype(BF16)
        to_send = jnp.concatenate([back[:, :width].astype(BF16), parts], axis=1)
        to_recv = jnp.concatenate([back[:, width : 2 * width].astype(BF16), parts], axis=1)
        own_s[...] += dot(rows_match(srow, nodes), to_send)
        away_s[...] += dot(rows_match(srow, away, nodes), to_send)
        recv_s[...] += dot(rows_match(rrow, nodes), to_recv)

    @pl.when((phase == 1) & (step == last))
    def _():
        gnode_ref[...] = agg_s[...] + own_s[:, :width] + recv_s[:, :width]
        moved = own_s[:, width:] - recv_s[:, width:]
        moved = moved + pltpu.roll(moved, 124, 1)
        gpos_ref[...] = jnp.where(lanes_like(moved) < 3, moved, 0.0)
        there = away_s[:, width:]
        there = there + pltpu.roll(there, 124, 1)
        there = jnp.where(lanes_like(there) < 3, there, 0.0)
        hi, lo = split(there)
        back_ref[:, :width] = away_s[:, :width].astype(BF16)
        back_ref[:, width:] = (hi.astype(F32) + pltpu.roll(lo.astype(F32), 4, 1)).astype(BF16)


def edges(senders, receivers, table, halo, edge_latent, edge_cot, node_cot, weights):
    block = 512
    count, width = edge_latent.shape
    turns = count // block
    nodes = table.shape[0]
    away = halo.shape[0]
    wide = table.shape[1]
    full = lambda shape: pl.BlockSpec(shape, lambda p, i: (0,) * len(shape))
    index_spec = pl.BlockSpec((1, 1, block), lambda p, i: (i, 0, 0))
    second = pl.BlockSpec((block, width), lambda p, i: (i * p, 0))
    return pl.pallas_call(
        edges_kernel,
        grid=(2, turns),
        in_specs=[
            index_spec,
            index_spec,
            full(table.shape),
            full(halo.shape),
            pl.BlockSpec((block, width), lambda p, i: (i * (1 - p), 0)),
            second,
            full(node_cot.shape),
        ]
        + [full(w.shape) for w in weights],
        out_specs=[second, full((nodes, width)), full((nodes, 128)), full((away, wide))],
        out_shape=[
            jax.ShapeDtypeStruct((count, width), F32),
            jax.ShapeDtypeStruct((nodes, width), F32),
            jax.ShapeDtypeStruct((nodes, 128), F32),
            jax.ShapeDtypeStruct((away, wide), BF16),
        ],
        scratch_shapes=[
            pltpu.VMEM((count, width), F32),
            pltpu.VMEM((count, width), F32),
            pltpu.VMEM((count, 128), F32),
            pltpu.VMEM((nodes, width), F32),
            pltpu.VMEM((nodes, width), BF16),
            pltpu.VMEM((384, width), BF16),
            pltpu.VMEM((128, 3 * width), BF16),
            pltpu.VMEM((nodes, wide), F32),
            pltpu.VMEM((away, wide), F32),
            pltpu.VMEM((nodes, wide), F32),
        ],
        compiler_params=pltpu.CompilerParams(
            dimension_semantics=("arbitrary", "arbitrary"), vmem_limit_bytes=58 * 1024 * 1024
        ),
        name="edges",
    )(
        senders.reshape(turns, 1, block),
        receivers.reshape(turns, 1, block),
        table,
        halo,
        edge_latent,
        edge_cot,
        node_cot,
        *weights,
    )


def finish_kernel(rows_ref, got_ref, gnode_ref, gpos_ref, pos_ref, cen_ref, out_ref, amp_ref, gp_s):
    width = gnode_ref.shape[1]

    @pl.when(pl.program_id(0) == 0)
    def _():
        back = dot(rows_match(rows_ref[...], gnode_ref.shape[0]), got_ref[...])
        out_ref[...] = gnode_ref[...] + back[:, :width]
        moved = back[:, width:]
        moved = gpos_ref[...] + (moved + pltpu.roll(moved, 124, 1))
        moved = jnp.where(lanes_like(moved) < 3, moved, 0.0)
        hi, lo = split(moved)
        gp_s[...] = (hi.astype(F32) + pltpu.roll(lo.astype(F32), 4, 1)).astype(BF16)

    cen = jnp.transpose(stack_rows([cen_ref[k : k + 1, :] for k in range(3)], 128))
    squared = None
    for k in range(3):
        off = pos_ref[k : k + 1, :] - cen[:, k : k + 1]
        squared = off * off if squared is None else squared + off * off
    phi_hi, phi_lo = split(jnp.exp(-RBF_RATE * squared))
    amp = dot(phi_hi, gp_s[...]) + dot(phi_lo, gp_s[...])
    amp = amp + pltpu.roll(amp, 124, 1)
    amp_ref[...] = jnp.transpose(amp)[:8, :]


def finish(rows, got, gnode, gpos, base_pos, centers):
    nodes, width = gnode.shape
    controls = centers.shape[1]
    block = 512
    full = lambda shape: pl.BlockSpec(shape, lambda i: (0,) * len(shape))
    return pl.pallas_call(
        finish_kernel,
        grid=(controls // block,),
        in_specs=[
            full(rows.shape),
            full(got.shape),
            full(gnode.shape),
            full(gpos.shape),
            full(base_pos.shape),
            pl.BlockSpec((3, block), lambda i: (0, i)),
        ],
        out_specs=[full(gnode.shape), pl.BlockSpec((8, block), lambda i: (0, i))],
        out_shape=[
            jax.ShapeDtypeStruct(gnode.shape, F32),
            jax.ShapeDtypeStruct((8, controls), F32),
        ],
        scratch_shapes=[pltpu.VMEM((nodes, 128), BF16)],
        compiler_params=pltpu.CompilerParams(dimension_semantics=("arbitrary",)),
        name="finish",
    )(rows, got, gnode, gpos, base_pos, centers)


def shards(
    node_latent,
    edge_latent,
    node_cot,
    edge_cot,
    base_pos,
    centers,
    amplitudes,
    edge_in,
    edge_geo,
    edge_out,
    edge_gain,
    node_in,
    node_out,
    node_gain,
    senders,
    receivers,
    send_rows,
):
    nodes = node_latent.shape[0]
    parts = lax.axis_size("dom")
    slots = send_rows.shape[2]
    me = lax.axis_index("dom")
    slot = jnp.maximum(senders - nodes, 0)
    off = slot // slots - me
    near = jnp.clip(jnp.where(off < 0, off + REACH, off + REACH - 1), 0, NEAR - 1)
    compact = jnp.where(senders >= nodes, nodes + near * slots + slot % slots, senders)
    twice = jnp.concatenate([send_rows[0], send_rows[0]], 0)
    around = lax.dynamic_slice_in_dim(twice, (me + parts - REACH) % parts, 2 * REACH + 1, 0)
    rows = jnp.concatenate([around[:REACH], around[REACH + 1 :]], 0).reshape(1, NEAR * slots)
    table, out = prepare(node_latent, base_pos, centers, amplitudes, rows)
    wide = table.shape[1]
    halo = exchange(out.reshape(NEAR, slots, wide), parts, 0).reshape(NEAR * slots, wide)
    weights = (
        edge_in,
        edge_geo,
        edge_out,
        edge_gain[None, :],
        node_in,
        node_out,
        node_gain[None, :],
    )
    grad_edges, gnode, gpos, back = edges(
        compact, receivers, table, halo, edge_latent, edge_cot, node_cot, weights
    )
    got = exchange(back.reshape(NEAR, slots, wide), parts, 1).reshape(NEAR * slots, wide)
    grad_nodes, amp = finish(rows, got, gnode, gpos, base_pos, centers)
    grad_controls = total(amp, parts, 2)[:3]
    return (grad_nodes, grad_edges, grad_controls)


def solution(mesh):
    split_rows = P(("groups", "dom"), None)
    in_specs = (
        split_rows,
        split_rows,
        split_rows,
        split_rows,
        P(None, ("groups", "dom")),
        P(),
        P(),
        P(),
        P(),
        P(),
        P(),
        P(),
        P(),
        P(),
        P(("groups", "dom")),
        P(("groups", "dom")),
        P(("groups", "dom"), None, None),
    )
    out_specs = (split_rows, split_rows, P("groups", None))
    return jax.shard_map(shards, mesh=mesh, in_specs=in_specs, out_specs=out_specs, check_vma=False)
```
